32 devices in a mesh: groups: 2 (over y), frame: 8 (over z, x), row: 2 (over core).
Axes of the slice: x: 2, y: 2, z: 4, core: 2. Of those that a mesh axis runs over, the one named last changes fastest.
Arguments:
- latent: bfloat16 [16, 16, 64, 640], P(('groups', 'frame'), 'row'), parts along dimension 0, may hold values from -18 to 18
- norm_gain: float32 [640], replicated, may hold values from 0.1 to 1.9
- time_kernel: bfloat16 [3, 640, 640], replicated, may hold values from -0.125 to 0.125
- space_norm: float32 [640], replicated, may hold values from 0.1 to 1.9
- space_qkv: bfloat16 [640, 1920], replicated, may hold values from -12 to 12
- space_out: bfloat16 [640, 640], replicated, may hold values from -0.25 to 0.25
- time_norm: float32 [640], replicated, may hold values from 0.1 to 1.9
- time_qkv: bfloat16 [640, 1920], replicated, may hold values from -12 to 12
- time_out: bfloat16 [640, 640], replicated, may hold values from -0.25 to 0.25
Outputs:
- output: float32 [16, 16, 64, 640], P(('groups', 'frame'), 'row'), parts along dimension 0
The draws below stay inside these ranges and needn't reach their ends.
There are 2 independent parts, one for each index of `groups`. The reference program is written for one: setup_inputs(seed, part) draws one part's arguments, and reference() takes and returns one part's arrays. A program takes and returns all parts, laid end to end along the dimension named above; an argument that names none is the same for every part. Nothing has to cross between parts.
All inputs are finite; a program needn't handle non-finite values.
Results may differ from the reference program's by a relative error of at most 0.0018.
Values may be sent and summed in bfloat16 or wider, within the bound.
A program may use at most 128 MiB of HBM per device.

```python
import jax
import jax.numpy as jnp
from jax import lax

C = 640
HEADS = 10
GROUPS = 32
WID = 64
FRAMES = 8
ROWS = 16


def projection_draw(key, salt):
    folded = jax.random.fold_in(key, salt)
    matrix = jax.random.normal(folded, (C, 3 * C), jnp.float32) / jnp.sqrt(jnp.float32(C))
    return jnp.clip(matrix, -12.0, 12.0).astype(jnp.bfloat16)


def draw_space_qkv(key, part):
    return projection_draw(key, 11)


def draw_time_qkv(key, part):
    return projection_draw(key, 23)


def draw_latent(key, part):
    folded = jax.random.fold_in(key, 37)
    offset_key = jax.random.fold_in(key, 41)
    sign_key = jax.random.fold_in(key, 43)
    position = jnp.arange(FRAMES, dtype=jnp.float32) / jnp.float32(max(FRAMES - 1, 1))
    magnitude = jax.random.uniform(offset_key, (GROUPS,), jnp.float32, 1.0, 2.5)
    signs = jnp.where(jax.random.uniform(sign_key, (GROUPS,), jnp.float32) < 0.5, -1.0, 1.0)
    group_offset = jnp.repeat(magnitude * signs, C // GROUPS)
    drift = (1.0 + 2.0 * position)[:, None, None, None] * group_offset[None, None, None, :]
    ramp = 1.0 + 2.0 * position
    values = jnp.clip(jax.random.normal(folded, (FRAMES, ROWS, WID, C), jnp.float32), -6.0, 6.0)
    return jnp.clip(values * ramp[:, None, None, None] + drift, -18.0, 18.0).astype(jnp.bfloat16)


def bell_draw(stream_key, dims, deviation, reach, kind=jnp.bfloat16):
    drawn = deviation * jax.random.normal(stream_key, dims, jnp.float32)
    return jnp.clip(drawn, min=-reach, max=reach).astype(kind)


def setup_inputs(seed: int = 0, part: int = 0) -> dict:
    key_list = jax.random.split(jax.random.key(seed), 10)
    part_splits = jax.random.split(jax.random.fold_in(key_list[9], part), 10)
    return {
        "latent": draw_latent(jax.random.fold_in(jax.random.fold_in(key_list[9], part), 71), part),
        "norm_gain": jnp.clip(1.0 + 0.18 * jax.random.normal(key_list[1], (C,), jnp.float32), 0.1, 1.9),
        "time_kernel": bell_draw(key_list[2], (3, C, C), (3 * C) ** -0.5, 0.125),
        "space_norm": jnp.clip(1.0 + 0.18 * jax.random.normal(key_list[3], (C,), jnp.float32), 0.1, 1.9),
        "space_qkv": draw_space_qkv(jax.random.fold_in(key_list[9], 71), part),
        "space_out": bell_draw(key_list[5], (C, C), C ** -0.5, 0.25),
        "time_norm": jnp.clip(1.0 + 0.18 * jax.random.normal(key_list[6], (C,), jnp.float32), 0.1, 1.9),
        "time_qkv": draw_time_qkv(jax.random.fold_in(key_list[9], 71), part),
        "time_out": bell_draw(key_list[8], (C, C), C ** -0.5, 0.25),
    }


epsilon = 1e-05

def normalize_silu(grouped, first, second, number, gain, shape):
    center = first / number
    spread = second / number - center * center
    scaling = lax.rsqrt(spread + epsilon)
    normed = ((grouped - center[:, None]) * scaling[:, None]).reshape(shape) * gain
    return jax.nn.silu(normed).astype(jnp.bfloat16)

def layer_norm(inputs, gain):
    widened = inputs.astype(jnp.float32)
    center = lax.optimization_barrier(jnp.mean(widened, axis=-1, keepdims=True))
    shifted = widened - center
    spread = lax.optimization_barrier(jnp.mean(shifted * shifted, axis=-1, keepdims=True))
    return (shifted * lax.rsqrt(spread + epsilon) * gain).astype(jnp.bfloat16)

def reference(latent, norm_gain, time_kernel, space_norm, space_qkv, space_out, time_norm, time_qkv, time_out):
    frames, row_count, col_count, channels = latent.shape
    pixels = row_count * col_count
    per_group = channels // GROUPS
    head_size = channels // HEADS
    scale = head_size ** (-0.5)
    grouped = latent.astype(jnp.float32).reshape(frames, row_count, col_count, GROUPS, per_group)
    first = lax.optimization_barrier(jnp.sum(grouped, axis=(0, 1, 2, 4)))
    second = lax.optimization_barrier(jnp.sum(grouped * grouped, axis=(0, 1, 2, 4)))
    number = frames * pixels * per_group
    hidden = normalize_silu(grouped, first, second, number, norm_gain, latent.shape)
    padded = jnp.pad(hidden, ((1, 1), (0, 0), (0, 0), (0, 0)))
    mixed = jnp.zeros((frames * pixels, channels), jnp.float32)
    for tap in range(3):
        window = padded[tap:tap + frames].reshape(-1, channels)
        mixed = mixed + jnp.dot(window, time_kernel[tap], preferred_element_type=jnp.float32)
    stepped = latent.astype(jnp.float32).reshape(-1, channels) + mixed
    tokens = layer_norm(stepped, space_norm)
    packed = jnp.dot(tokens, space_qkv, preferred_element_type=jnp.float32).astype(jnp.bfloat16)
    packed = packed.reshape(frames, pixels, 3, HEADS, head_size)

    def one_frame(block):
        queries = block[:, 0].astype(jnp.float32)
        key_rows = block[:, 1].astype(jnp.float32)
        values = block[:, 2].astype(jnp.float32)
        scores = jnp.einsum('qhd,khd->hqk', queries, key_rows) * scale
        raised = jnp.exp(scores - lax.optimization_barrier(jnp.max(scores, axis=-1, keepdims=True)))
        weight_sum = lax.optimization_barrier(jnp.sum(raised, axis=-1))
        weights = raised.astype(jnp.bfloat16).astype(jnp.float32)
        result = jnp.einsum('hqk,khd->qhd', weights, values) / jnp.transpose(weight_sum)[:, :, None]
        return result.astype(jnp.bfloat16).reshape(pixels, channels)
    attended = lax.map(one_frame, packed)
    spaced = stepped + jnp.dot(attended.reshape(-1, channels), space_out, preferred_element_type=jnp.float32)
    normed = layer_norm(spaced, time_norm)
    packed_time = jnp.dot(normed, time_qkv, preferred_element_type=jnp.float32).astype(jnp.bfloat16)
    packed_time = packed_time.reshape(frames, pixels, 3, HEADS, head_size).astype(jnp.float32)
    queries = packed_time[:, :, 0]
    key_rows = packed_time[:, :, 1]
    values = packed_time[:, :, 2]
    scores = jnp.einsum('qphd,kphd->phqk', queries, key_rows) * scale
    raised = jnp.exp(scores - lax.optimization_barrier(jnp.max(scores, axis=-1, keepdims=True)))
    weight_sum = lax.optimization_barrier(jnp.sum(raised, axis=-1))
    weights = raised.astype(jnp.bfloat16).astype(jnp.float32)
    result = jnp.einsum('phqk,kphd->qphd', weights, values) / jnp.transpose(weight_sum, (2, 0, 1))[:, :, :, None]
    attended_time = result.astype(jnp.bfloat16).reshape(-1, channels)
    output = spaced + jnp.dot(attended_time, time_out, preferred_element_type=jnp.float32)
    return output.reshape(frames, row_count, col_count, channels)
```

```python
import jax
import jax.numpy as jnp
from jax import lax
from jax.sharding import PartitionSpec as P

HEADS = 10
GROUPS = 32


epsilon = 1e-05


def padded_2(block, sides, width):
    for axis, dim in sides:
        count = lax.axis_size(axis)
        forward = [(i, i + 1) for i in range(count - 1)]
        backward = [(target, source) for source, target in forward]
        low = lax.ppermute(
            lax.slice_in_dim(block, block.shape[dim] - width, None, axis=dim), axis, forward
        )
        high = lax.ppermute(lax.slice_in_dim(block, 0, width, axis=dim), axis, backward)
        block = jnp.concatenate([low, block, high], axis=dim)
    return block


def normalize_silu(grouped, first, second, number, gain, shape):
    center = first / number
    spread = second / number - center * center
    scaling = lax.rsqrt(spread + epsilon)
    normed = ((grouped - center[:, None]) * scaling[:, None]).reshape(shape) * gain
    return jax.nn.silu(normed).astype(jnp.bfloat16)


def layer_norm(inputs, gain):
    center = jnp.mean(inputs, axis=-1, keepdims=True)
    shifted = inputs - center
    spread = jnp.mean(shifted * shifted, axis=-1, keepdims=True)
    return (shifted * lax.rsqrt(spread + epsilon) * gain).astype(jnp.bfloat16)


def project_three(inputs, weight):
    channels = weight.shape[0]
    lead = inputs.shape[:-1]
    packed = jnp.dot(
        inputs.reshape(-1, channels), weight, preferred_element_type=jnp.float32
    ).astype(jnp.bfloat16)
    packed = packed.reshape(lead + (3 * channels,))
    return (
        packed[..., :channels],
        packed[..., channels : 2 * channels],
        packed[..., 2 * channels :],
    )


def time_attend(queries, key_rows, values):
    frames, pixels, channels = queries.shape
    head_size = channels // HEADS
    query_heads = queries.reshape(frames, pixels, HEADS, head_size)
    key_heads = key_rows.reshape(frames, pixels, HEADS, head_size)
    value_heads = values.reshape(frames, pixels, HEADS, head_size)
    scores = jnp.einsum(
        "qphd,kphd->phqk", query_heads, key_heads, preferred_element_type=jnp.float32
    ) * head_size ** (-0.5)
    raised = jnp.exp(scores - jnp.max(scores, axis=-1, keepdims=True))
    weight_sum = jnp.sum(raised, axis=-1)
    weights = raised.astype(jnp.bfloat16)
    result = jnp.einsum("phqk,kphd->qphd", weights, value_heads, preferred_element_type=jnp.float32)
    result = result / jnp.transpose(weight_sum, (2, 0, 1))[:, :, :, None]
    return result.astype(jnp.bfloat16).reshape(frames, pixels, channels)


def add_projected(base, attended, weight):
    channels = weight.shape[0]
    summed = base.reshape(-1, channels) + jnp.dot(
        attended.reshape(-1, channels), weight, preferred_element_type=jnp.float32
    )
    return summed.reshape(base.shape)


def body(
    latent, norm_gain, time_kernel, space_norm, space_qkv, space_out, time_norm, time_qkv, time_out
):
    frames, row_count, col_count, channels = latent.shape
    pixels = row_count * col_count
    per_group = channels // GROUPS
    head_size = channels // HEADS
    grouped = latent.astype(jnp.float32).reshape(frames, row_count, col_count, GROUPS, per_group)
    first = jnp.sum(grouped, axis=(0, 1, 2, 4))
    second = jnp.sum(grouped * grouped, axis=(0, 1, 2, 4))
    first, second = lax.psum((first, second), ("frame", "row"))
    number = frames * lax.axis_size("frame") * pixels * lax.axis_size("row") * per_group
    wide = padded_2(latent, (("frame", 0),), 1)
    wide_frames = wide.shape[0]
    wide_grouped = wide.astype(jnp.float32).reshape(
        wide_frames, row_count, col_count, GROUPS, per_group
    )
    padded = normalize_silu(wide_grouped, first, second, number, norm_gain, wide.shape)
    me, count = lax.axis_index("frame"), lax.axis_size("frame")
    place = me * frames - 1 + jnp.arange(wide_frames)
    inside = (place >= 0) & (place < count * frames)
    padded = jnp.where(inside[:, None, None, None], padded, jnp.zeros((), padded.dtype))
    mixed = jnp.zeros((frames * pixels, channels), jnp.float32)
    for tap in range(3):
        window = padded[tap : tap + frames].reshape(-1, channels)
        mixed = mixed + jnp.dot(window, time_kernel[tap], preferred_element_type=jnp.float32)
    stepped = latent.astype(jnp.float32).reshape(-1, channels) + mixed
    stepped = stepped.reshape(frames, pixels, channels)
    tokens = layer_norm(stepped, space_norm)
    queries, key_rows, values = project_three(tokens, space_qkv)
    query_heads = queries.reshape(frames, pixels, HEADS, head_size)
    top_score = jnp.full((frames, HEADS, pixels), -jnp.inf, jnp.float32)
    weight_sum = jnp.zeros((frames, HEADS, pixels), jnp.float32)
    partial_sum = jnp.zeros((frames, HEADS, pixels, head_size), jnp.float32)
    key_piece = lax.all_gather(key_rows, "row", axis=1, tiled=True)
    value_piece = lax.all_gather(values, "row", axis=1, tiled=True)
    key_count = key_piece.shape[1]
    key_heads = key_piece.reshape(frames, key_count, HEADS, head_size)
    value_heads = value_piece.reshape(frames, key_count, HEADS, head_size)
    scores = jnp.einsum(
        "fqhd,fkhd->fhqk", query_heads, key_heads, preferred_element_type=jnp.float32
    ) * head_size ** (-0.5)
    new_top = jnp.max(scores, axis=-1)
    rescale = jnp.exp(top_score - new_top)
    raised = jnp.exp(scores - new_top[..., None])
    weight_sum = weight_sum * rescale + jnp.sum(raised, axis=-1)
    weights = raised.astype(jnp.bfloat16)
    partial_sum = partial_sum * rescale[..., None] + jnp.einsum(
        "fhqk,fkhd->fhqd", weights, value_heads, preferred_element_type=jnp.float32
    )
    top_score, weight_sum, partial_sum = (new_top, weight_sum, partial_sum)
    attended = (partial_sum / weight_sum[..., None]).astype(jnp.bfloat16)
    attended = jnp.transpose(attended, (0, 2, 1, 3)).reshape(frames, pixels, channels)
    spaced = add_projected(stepped, attended, space_out)
    normed = layer_norm(spaced, time_norm)
    moved = lax.all_to_all(normed, "frame", split_axis=1, concat_axis=0, tiled=True)
    queries, key_rows, values = project_three(moved, time_qkv)
    result = time_attend(queries, key_rows, values)
    result = lax.all_to_all(result, "frame", split_axis=0, concat_axis=1, tiled=True)
    output = add_projected(spaced, result, time_out)
    return output.reshape(frames, row_count, col_count, channels)


def solution(mesh):
    return jax.shard_map(
        body,
        mesh=mesh,
        in_specs=(
            P(("groups", "frame"), "row", None, None),
            P(),
            P(),
            P(),
            P(),
            P(),
            P(),
            P(),
            P(),
        ),
        out_specs=P(("groups", "frame"), "row", None, None),
        check_vma=False,
    )
```

```python
import functools

import jax
import jax.numpy as jnp
from jax import lax
from jax.experimental import pallas as pl
from jax.experimental.pallas import tpu as pltpu
from jax.sharding import PartitionSpec as P

HEADS = 10
GROUPS = 32
MESH = pl.DeviceIdType.MESH
F32 = jnp.float32
BF16 = jnp.bfloat16

epsilon = 1e-05


def layer_norm(inputs, gain):
    center = jnp.mean(inputs, axis=-1, keepdims=True)
    shifted = inputs - center
    spread = jnp.mean(shifted * shifted, axis=-1, keepdims=True)
    return (shifted * lax.rsqrt(spread + epsilon) * gain).astype(BF16)


def dot(a, b):
    return jnp.dot(a, b, preferred_element_type=F32)


def dot_nt(a, b):
    return lax.dot_general(a, b, (((1,), (1,)), ((), ())), preferred_element_type=F32)


def kernel(
    frames, rows, chunks, number,
    latent, norm_gain, group_ones, time_kernel, space_norm, space_qkv, space_out, time_norm, time_qkv, time_out,
    out,
    own, near, far, stepped, tok_own, tok_other, q_all, k_all, v_all, nbuf, rbuf, abuf, obuf, part, stats,
    w_conv, w_sqkv, w_sout, w_tqkv, w_tout, att, q2, k2, v2, hid_scale,
    w_sem, stat_send, stat_recv, near_send, near_recv, far_send, far_recv, tok_send, tok_recv,
    fwd_send, fwd_recv, back_send, back_recv,
):
    me = lax.axis_index("frame")
    row = lax.axis_index("row")
    pixels, channels = own.shape
    size = pixels // chunks
    per = size // frames
    head = channels // HEADS
    pairs = HEADS // 2
    devices = frames * rows
    mine = me * rows + row
    odd = lax.rem(me, 2)
    partner = me + 1 - 2 * odd
    relay_to = me + 2 - 4 * odd
    far_from = me - 2 + 4 * odd
    relays = jnp.logical_and(relay_to >= 0, relay_to < frames)
    has_far = jnp.logical_and(far_from >= 0, far_from < frames)

    copies = [
        pltpu.make_async_copy(latent, own, w_sem.at[0]),
        pltpu.make_async_copy(time_kernel.at[1], w_conv.at[0], w_sem.at[1]),
        pltpu.make_async_copy(time_kernel.at[2 - 2 * odd], w_conv.at[1], w_sem.at[2]),
        pltpu.make_async_copy(time_kernel.at[2 * odd], w_conv.at[2], w_sem.at[3]),
        pltpu.make_async_copy(space_qkv, w_sqkv, w_sem.at[4]),
        pltpu.make_async_copy(space_out, w_sout, w_sem.at[5]),
        pltpu.make_async_copy(time_qkv, w_tqkv, w_sem.at[6]),
        pltpu.make_async_copy(time_out, w_tout, w_sem.at[7]),
    ]
    for copy in copies:
        copy.start()

    barrier = pltpu.get_barrier_semaphore()

    @pl.loop(1, devices)
    def _(i):
        peer = lax.rem(mine + i, devices)
        pl.semaphore_signal(
            barrier, inc=1, device_id={"frame": peer // rows, "row": lax.rem(peer, rows)}, device_id_type=MESH
        )

    copies[0].wait()
    first = jnp.zeros((1, channels), F32)
    second = jnp.zeros((1, channels), F32)
    for c in range(chunks):
        block = own[c * size : (c + 1) * size, :].astype(F32)
        first = first + jnp.sum(block, axis=0, keepdims=True)
        second = second + jnp.sum(block * block, axis=0, keepdims=True)
    part[...] = jnp.concatenate([first, second, jnp.zeros((6, channels), F32)], axis=0)
    pl.semaphore_wait(barrier, devices - 1)

    def near_copy(j):
        at = pl.ds(j * size, size)
        return pltpu.make_async_remote_copy(
            latent.at[at], near.at[at], near_send.at[j], near_recv.at[j],
            device_id={"frame": partner}, device_id_type=MESH,
        )

    def far_copy(j):
        at = pl.ds(j * size, size)
        return pltpu.make_async_remote_copy(
            near.at[at], far.at[at], far_send.at[j], far_recv.at[j],
            device_id={"frame": lax.max(0, lax.min(relay_to, frames - 1))}, device_id_type=MESH,
        )

    def tok_copy(j):
        at = pl.ds(j * size, size)
        return pltpu.make_async_remote_copy(
            tok_own.at[at], tok_other.at[at], tok_send.at[j], tok_recv.at[j],
            device_id={"row": 1 - row}, device_id_type=MESH,
        )

    def stat_copy(peer, slot):
        return pltpu.make_async_remote_copy(
            part, stats.at[slot], stat_send.at[peer], stat_recv.at[slot],
            device_id={"frame": peer // rows, "row": lax.rem(peer, rows)}, device_id_type=MESH,
        )

    @pl.loop(1, devices)
    def _(i):
        peer = lax.rem(mine + i, devices)
        stat_copy(peer, mine).start()

    @pl.loop(0, chunks)
    def _(j):
        near_copy(j).start()

    stats[mine] = part[...]

    @pl.loop(1, devices)
    def _(i):
        source = lax.rem(mine + i, devices)
        stat_copy(source, source).wait_recv()

    total = jnp.sum(stats[...], axis=0)
    grouped = jnp.dot(total, group_ones[...], preferred_element_type=F32, precision=lax.Precision.HIGHEST)
    center = grouped[0:1] / number
    spread = grouped[1:2] / number - center * center
    hid_scale[0:1, :] = center
    hid_scale[1:2, :] = lax.rsqrt(spread + epsilon) * norm_gain[...]

    def hidden(ref, c):
        block = ref[pl.ds(c * size, size), :].astype(F32)
        v = (block - hid_scale[0:1, :]) * hid_scale[1:2, :]
        return (v / (1.0 + jnp.exp(-v))).astype(BF16)

    copies[1].wait()

    @pl.loop(0, chunks)
    def _(c):
        at = pl.ds(c * size, size)
        stepped[at, :] = own[at, :].astype(F32) + dot(hidden(own, c), w_conv[0])

    for copy in copies[2:6]:
        copy.wait()

    scale = head ** (-0.5)

    @pl.loop(0, chunks + 1)
    def _(t):
        @pl.when(t < chunks)
        def _():
            near_copy(t).wait_recv()

            @pl.when(relays)
            def _():
                far_copy(t).start()

            at = pl.ds(t * size, size)
            stepped[at, :] += dot(hidden(near, t), w_conv[1])

        @pl.when(t >= 1)
        def _():
            c = t - 1
            at = pl.ds(c * size, size)

            @pl.when(has_far)
            def _():
                far_copy(c).wait_recv()
                stepped[at, :] += dot(hidden(far, c), w_conv[2])

            tok_own[at, :] = layer_norm(stepped[at, :], space_norm[...])
            tok_copy(c).start()
            tokens = tok_own[at, :]
            q_all[at, :] = (dot(tokens, w_sqkv[:, :channels]) * scale).astype(BF16)
            k_all[at, :] = dot(tokens, w_sqkv[:, channels : 2 * channels]).astype(BF16)
            v_all[at, :] = dot(tokens, w_sqkv[:, 2 * channels :]).astype(BF16)

    @pl.loop(0, chunks)
    def _(c):
        tok_copy(c).wait_recv()
        tokens = tok_other[pl.ds(c * size, size), :]
        to = pl.ds(pixels + c * size, size)
        k_all[to, :] = dot(tokens, w_sqkv[:, channels : 2 * channels]).astype(BF16)
        v_all[to, :] = dot(tokens, w_sqkv[:, 2 * channels :]).astype(BF16)

    for copy in copies[6:]:
        copy.wait()

    lane = lax.broadcasted_iota(jnp.int32, (1, 2 * head), 1)
    low = lane < head
    masks = (low.astype(F32).astype(BF16), (1.0 - low.astype(F32)).astype(BF16))

    def attend_pair(query, keys, values, same):
        results = []
        for mask in masks:
            scores = dot_nt(query * mask, keys)
            if same is not None:
                scores = jnp.where(same, scores, -jnp.inf)
            raised = jnp.exp(scores - jnp.max(scores, axis=-1, keepdims=True))
            weight_sum = jnp.sum(raised, axis=-1, keepdims=True)
            results.append(dot(raised.astype(BF16), values) / weight_sum)
        return jnp.where(low, results[0], results[1]).astype(BF16)

    def slot(c, f):
        return pl.ds(pl.multiple_of(c * size + f * per, per), per)

    def fwd_copy(c, dest, source):
        return pltpu.make_async_remote_copy(
            nbuf.at[slot(c, dest)], rbuf.at[slot(c, source)],
            fwd_send.at[c, dest], fwd_recv.at[c, source],
            device_id={"frame": dest}, device_id_type=MESH,
        )

    def back_copy(c, dest, source):
        return pltpu.make_async_remote_copy(
            abuf.at[slot(c, dest)], obuf.at[slot(c, source)],
            back_send.at[c, dest], back_recv.at[c, source],
            device_id={"frame": dest}, device_id_type=MESH,
        )

    @pl.loop(0, chunks + 2)
    def _(t):
        @pl.when(t < chunks)
        def _():
            c = t
            at = pl.ds(c * size, size)
            for p in range(pairs):
                block = slice(p * 2 * head, (p + 1) * 2 * head)
                att[:, block] = attend_pair(q_all[at, block], k_all[:, block], v_all[:, block], None)
            spaced = stepped[at, :] + dot(att[...], w_sout[...])
            stepped[at, :] = spaced
            nbuf[at, :] = layer_norm(spaced, time_norm[...])

            @pl.loop(1, frames)
            def _(i):
                fwd_copy(c, lax.rem(me + i, frames), me).start()

            rbuf[slot(c, me), :] = nbuf[slot(c, me), :]

        @pl.when(jnp.logical_and(t >= 1, t <= chunks))
        def _():
            c = t - 1
            at = pl.ds(c * size, size)

            @pl.loop(1, frames)
            def _(i):
                source = lax.rem(me + i, frames)
                fwd_copy(c, source, source).wait_recv()

            tokens = rbuf[at, :]
            q2[...] = (dot(tokens, w_tqkv[:, :channels]) * scale).astype(BF16)
            k2[...] = dot(tokens, w_tqkv[:, channels : 2 * channels]).astype(BF16)
            v2[...] = dot(tokens, w_tqkv[:, 2 * channels :]).astype(BF16)
            across = lax.broadcasted_iota(jnp.int32, (size, size), 1)
            down = lax.broadcasted_iota(jnp.int32, (size, size), 0)
            same = lax.rem(across, per) == lax.rem(down, per)
            for p in range(pairs):
                block = slice(p * 2 * head, (p + 1) * 2 * head)
                abuf[at, block] = attend_pair(q2[:, block], k2[:, block], v2[:, block], same)

            @pl.loop(1, frames)
            def _(i):
                back_copy(c, lax.rem(me + i, frames), me).start()

            obuf[slot(c, me), :] = abuf[slot(c, me), :]

        @pl.when(t >= 2)
        def _():
            c = t - 2
            at = pl.ds(c * size, size)

            @pl.loop(1, frames)
            def _(i):
                source = lax.rem(me + i, frames)
                back_copy(c, source, source).wait_recv()

            out[at, :] = stepped[at, :] + dot(obuf[at, :], w_tout[...])

    @pl.loop(1, devices)
    def _(i):
        peer = lax.rem(mine + i, devices)
        stat_copy(peer, mine).wait_send()

    @pl.loop(0, chunks)
    def _(c):
        near_copy(c).wait_send()
        tok_copy(c).wait_send()

        @pl.when(relays)
        def _():
            far_copy(c).wait_send()

        @pl.loop(1, frames)
        def _(i):
            dest = lax.rem(me + i, frames)
            fwd_copy(c, dest, me).wait_send()
            back_copy(c, dest, me).wait_send()


def body(
    frames, rows,
    latent, norm_gain, time_kernel, space_norm, space_qkv, space_out, time_norm, time_qkv, time_out,
):
    held, row_count, col_count, channels = latent.shape
    pixels = held * row_count * col_count
    per_group = channels // GROUPS
    chunks = max(1, pixels // (16 * frames))
    size = pixels // chunks
    number = float(frames * rows * pixels * per_group)
    group = jnp.arange(channels) // per_group
    group_ones = (group[:, None] == group[None, :]).astype(F32)
    devices = frames * rows
    vmem = pl.BlockSpec(memory_space=pltpu.VMEM)
    hbm = pl.BlockSpec(memory_space=pl.ANY)

    def wide(n=pixels, kind=BF16, width=channels):
        return pltpu.VMEM((n, width), kind)

    dma = pltpu.SemaphoreType.DMA
    output = pl.pallas_call(
        functools.partial(kernel, frames, rows, chunks, number),
        out_shape=jax.ShapeDtypeStruct((pixels, channels), F32),
        in_specs=[hbm, vmem, vmem, hbm, vmem, hbm, hbm, vmem, hbm, hbm],
        out_specs=vmem,
        scratch_shapes=[
            wide(), wide(), wide(), wide(kind=F32), wide(), wide(), wide(), wide(2 * pixels), wide(2 * pixels),
            wide(), wide(), wide(), wide(),
            pltpu.VMEM((8, channels), F32),
            pltpu.VMEM((devices, 8, channels), F32),
            pltpu.VMEM((3, channels, channels), BF16),
            wide(channels, BF16, 3 * channels), wide(channels),
            wide(channels, BF16, 3 * channels), wide(channels),
            wide(size), wide(size), wide(size), wide(size),
            pltpu.VMEM((8, channels), F32),
            dma((8,)), dma((devices,)), dma((devices,)),
            dma((chunks,)), dma((chunks,)), dma((chunks,)), dma((chunks,)), dma((chunks,)), dma((chunks,)),
            dma((chunks, frames)), dma((chunks, frames)), dma((chunks, frames)), dma((chunks, frames)),
        ],
        compiler_params=pltpu.CompilerParams(
            collective_id=0, has_side_effects=True, vmem_limit_bytes=60 * 1024 * 1024
        ),
    )(
        latent.reshape(pixels, channels), norm_gain[None], group_ones, time_kernel, space_norm[None], space_qkv,
        space_out, time_norm[None], time_qkv, time_out,
    )
    return output.reshape(latent.shape)


def solution(mesh):
    frames, rows = mesh.shape["frame"], mesh.shape["row"]
    split = P(("groups", "frame"), "row", None, None)
    return jax.shard_map(
        functools.partial(body, frames, rows),
        mesh=mesh,
        in_specs=(split, P(), P(), P(), P(), P(), P(), P(), P()),
        out_specs=split,
        check_vma=False,
    )
```

```python
import functools

import jax
import jax.numpy as jnp
from jax import lax
from jax.experimental import pallas as pl
from jax.experimental.pallas import tpu as pltpu
from jax.sharding import PartitionSpec as P

HEADS = 10
GROUPS = 32
MESH = pl.DeviceIdType.MESH
F32 = jnp.float32
BF16 = jnp.bfloat16

epsilon = 1e-05


def layer_norm(inputs, gain):
    center = jnp.mean(inputs, axis=-1, keepdims=True)
    shifted = inputs - center
    spread = jnp.mean(shifted * shifted, axis=-1, keepdims=True)
    return (shifted * lax.rsqrt(spread + epsilon) * gain).astype(BF16)


def dot(a, b):
    return jnp.dot(a, b, preferred_element_type=F32)


def dot_nt(a, b):
    return lax.dot_general(a, b, (((1,), (1,)), ((), ())), preferred_element_type=F32)


def kernel(
    frames, rows, chunks, number, per_group,
    latent, norm_gain, time_kernel, space_norm, space_qkv, space_out, time_norm, time_qkv, time_out,
    out,
    own, near, far, stepped, tok_own, tok_other, q_all, k_all, v_all, nbuf, rbuf, abuf, obuf, part, stats,
    w_conv, w_sqkv, w_sout, w_tqkv, w_tout, att, q2, k2, v2, hid_scale, group_ones,
    w_sem, stat_send, stat_recv, near_send, near_recv, far_send, far_recv, tok_send, tok_recv,
    fwd_send, fwd_recv, back_send, back_recv, out_sem,
):
    me = lax.axis_index("frame")
    row = lax.axis_index("row")
    pixels, channels = own.shape
    size = pixels // chunks
    per = size // frames
    head = channels // HEADS
    pairs = HEADS // 2
    devices = frames * rows
    mine = me * rows + row
    odd = lax.rem(me, 2)
    partner = me + 1 - 2 * odd
    relay_to = me + 2 - 4 * odd
    far_from = me - 2 + 4 * odd
    relays = jnp.logical_and(relay_to >= 0, relay_to < frames)
    has_far = jnp.logical_and(far_from >= 0, far_from < frames)

    copies = [
        pltpu.make_async_copy(latent, own, w_sem.at[0]),
        pltpu.make_async_copy(time_kernel.at[1], w_conv.at[0], w_sem.at[1]),
        pltpu.make_async_copy(time_kernel.at[2 - 2 * odd], w_conv.at[1], w_sem.at[2]),
        pltpu.make_async_copy(time_kernel.at[2 * odd], w_conv.at[2], w_sem.at[3]),
        pltpu.make_async_copy(space_qkv, w_sqkv, w_sem.at[4]),
        pltpu.make_async_copy(space_out, w_sout, w_sem.at[5]),
        pltpu.make_async_copy(time_qkv, w_tqkv, w_sem.at[6]),
        pltpu.make_async_copy(time_out, w_tout, w_sem.at[7]),
    ]
    for copy in copies:
        copy.start()

    barrier = pltpu.get_barrier_semaphore()

    @pl.loop(1, devices)
    def _(i):
        peer = lax.rem(mine + i, devices)
        pl.semaphore_signal(
            barrier, inc=1, device_id={"frame": peer // rows, "row": lax.rem(peer, rows)}, device_id_type=MESH
        )

    copies[0].wait()
    first = jnp.zeros((1, channels), F32)
    second = jnp.zeros((1, channels), F32)
    for c in range(chunks):
        block = own[c * size : (c + 1) * size, :].astype(F32)
        first = first + jnp.sum(block, axis=0, keepdims=True)
        second = second + jnp.sum(block * block, axis=0, keepdims=True)
    part[...] = jnp.concatenate([first, second, jnp.zeros((6, channels), F32)], axis=0)
    down = lax.broadcasted_iota(jnp.int32, (channels, channels), 0)
    start = down - lax.rem(down, per_group)
    across = lax.broadcasted_iota(jnp.int32, (channels, channels), 1)
    inside = jnp.logical_and(across >= start, across < start + per_group)
    group_ones[...] = jnp.where(inside, 1.0, 0.0).astype(BF16)
    pl.semaphore_wait(barrier, devices - 1)

    def near_copy(j):
        at = pl.ds(j * size, size)
        return pltpu.make_async_remote_copy(
            latent.at[at], near.at[at], near_send.at[j], near_recv.at[j],
            device_id={"frame": partner}, device_id_type=MESH,
        )

    def far_copy(j):
        at = pl.ds(j * size, size)
        return pltpu.make_async_remote_copy(
            near.at[at], far.at[at], far_send.at[j], far_recv.at[j],
            device_id={"frame": lax.max(0, lax.min(relay_to, frames - 1))}, device_id_type=MESH,
        )

    def tok_copy(j):
        at = pl.ds(j * size, size)
        return pltpu.make_async_remote_copy(
            tok_own.at[at], tok_other.at[at], tok_send.at[j], tok_recv.at[j],
            device_id={"row": 1 - row}, device_id_type=MESH,
        )

    def stat_copy(peer, slot):
        return pltpu.make_async_remote_copy(
            part, stats.at[slot], stat_send.at[peer], stat_recv.at[slot],
            device_id={"frame": peer // rows, "row": lax.rem(peer, rows)}, device_id_type=MESH,
        )

    @pl.loop(1, devices)
    def _(i):
        peer = lax.rem(mine + i, devices)
        stat_copy(peer, mine).start()

    @pl.loop(0, chunks)
    def _(j):
        near_copy(j).start()

    stats[mine] = part[...]

    @pl.loop(1, devices)
    def _(i):
        source = lax.rem(mine + i, devices)
        stat_copy(source, source).wait_recv()

    total = jnp.sum(stats[...], axis=0)
    high = total.astype(BF16).astype(F32)
    middle = (total - high).astype(BF16).astype(F32)
    lowest = total - high - middle
    pieces = dot(jnp.concatenate([high, middle, lowest], axis=0).astype(BF16), group_ones[...])
    grouped = pieces[0:8] + pieces[8:16] + pieces[16:24]
    center = grouped[0:1] / number
    spread = grouped[1:2] / number - center * center
    hid_scale[0:1, :] = center
    hid_scale[1:2, :] = lax.rsqrt(spread + epsilon) * norm_gain[...].reshape(1, channels)

    def hidden(ref, c):
        block = ref[pl.ds(c * size, size), :].astype(F32)
        v = (block - hid_scale[0:1, :]) * hid_scale[1:2, :]
        return (v / (1.0 + jnp.exp(-v))).astype(BF16)

    copies[1].wait()

    @pl.loop(0, chunks)
    def _(c):
        at = pl.ds(c * size, size)
        stepped[at, :] = own[at, :].astype(F32) + dot(hidden(own, c), w_conv[0])

    for copy in copies[2:6]:
        copy.wait()

    scale = head ** (-0.5)

    @pl.loop(0, chunks + 2)
    def _(t):
        @pl.when(t < chunks)
        def _():
            near_copy(t).wait_recv()

            @pl.when(relays)
            def _():
                far_copy(t).start()

            at = pl.ds(t * size, size)
            stepped[at, :] += dot(hidden(near, t), w_conv[1])

        @pl.when(jnp.logical_and(t >= 1, t <= chunks))
        def _():
            c = t - 1
            at = pl.ds(c * size, size)

            @pl.when(has_far)
            def _():
                far_copy(c).wait_recv()
                stepped[at, :] += dot(hidden(far, c), w_conv[2])

            tok_own[at, :] = layer_norm(stepped[at, :], space_norm[...].reshape(1, channels))
            tok_copy(c).start()
            tokens = tok_own[at, :]
            q_all[at, :] = (dot(tokens, w_sqkv[:, :channels]) * scale).astype(BF16)
            k_all[at, :] = dot(tokens, w_sqkv[:, channels : 2 * channels]).astype(BF16)
            v_all[at, :] = dot(tokens, w_sqkv[:, 2 * channels :]).astype(BF16)

        @pl.when(t >= 2)
        def _():
            c = t - 2
            tok_copy(c).wait_recv()
            tokens = tok_other[pl.ds(c * size, size), :]
            to = pl.ds(pixels + c * size, size)
            k_all[to, :] = dot(tokens, w_sqkv[:, channels : 2 * channels]).astype(BF16)
            v_all[to, :] = dot(tokens, w_sqkv[:, 2 * channels :]).astype(BF16)

    for copy in copies[6:]:
        copy.wait()

    lane = lax.broadcasted_iota(jnp.int32, (1, 2 * head), 1)
    low = lane < head
    masks = (low.astype(F32).astype(BF16), (1.0 - low.astype(F32)).astype(BF16))

    def attend_pair(query, keys, values, same):
        both = jnp.concatenate([query * mask for mask in masks], axis=0)
        scores = dot_nt(both, keys)
        if same is not None:
            scores = jnp.where(same, scores, -jnp.inf)
        raised = jnp.exp(scores - jnp.max(scores, axis=-1, keepdims=True))
        weight_sum = jnp.sum(raised, axis=-1, keepdims=True)
        result = dot(raised.astype(BF16), values) / weight_sum
        return jnp.where(low, result[:size], result[size:]).astype(BF16)

    def slot(c, f):
        return pl.ds(pl.multiple_of(c * size + f * per, per), per)

    def fwd_copy(c, dest, source):
        return pltpu.make_async_remote_copy(
            nbuf.at[slot(c, dest)], rbuf.at[slot(c, source)],
            fwd_send.at[c, dest], fwd_recv.at[c, source],
            device_id={"frame": dest}, device_id_type=MESH,
        )

    def out_copy(c):
        at = pl.ds(c * size, size)
        return pltpu.make_async_copy(stepped.at[at], out.at[at], out_sem.at[c])

    def back_copy(c, dest, source):
        return pltpu.make_async_remote_copy(
            abuf.at[slot(c, dest)], obuf.at[slot(c, source)],
            back_send.at[c, dest], back_recv.at[c, source],
            device_id={"frame": dest}, device_id_type=MESH,
        )

    @pl.loop(0, chunks + 2)
    def _(t):
        @pl.when(t < chunks)
        def _():
            c = t
            at = pl.ds(c * size, size)
            for p in range(pairs):
                block = slice(p * 2 * head, (p + 1) * 2 * head)
                att[:, block] = attend_pair(q_all[at, block], k_all[:, block], v_all[:, block], None)
            spaced = stepped[at, :] + dot(att[...], w_sout[...])
            stepped[at, :] = spaced
            nbuf[at, :] = layer_norm(spaced, time_norm[...].reshape(1, channels))

            @pl.loop(1, frames)
            def _(i):
                fwd_copy(c, lax.rem(me + i, frames), me).start()

            rbuf[slot(c, me), :] = nbuf[slot(c, me), :]

        @pl.when(jnp.logical_and(t >= 1, t <= chunks))
        def _():
            c = t - 1
            at = pl.ds(c * size, size)

            @pl.loop(1, frames)
            def _(i):
                source = lax.rem(me + i, frames)
                fwd_copy(c, source, source).wait_recv()

            tokens = rbuf[at, :]
            q2[...] = (dot(tokens, w_tqkv[:, :channels]) * scale).astype(BF16)
            k2[...] = dot(tokens, w_tqkv[:, channels : 2 * channels]).astype(BF16)
            v2[...] = dot(tokens, w_tqkv[:, 2 * channels :]).astype(BF16)
            across = lax.broadcasted_iota(jnp.int32, (2 * size, size), 1)
            down = lax.broadcasted_iota(jnp.int32, (2 * size, size), 0)
            same = lax.rem(across, per) == lax.rem(down, per)
            for p in range(pairs):
                block = slice(p * 2 * head, (p + 1) * 2 * head)
                abuf[at, block] = attend_pair(q2[:, block], k2[:, block], v2[:, block], same)

            @pl.loop(1, frames)
            def _(i):
                back_copy(c, lax.rem(me + i, frames), me).start()

            obuf[slot(c, me), :] = abuf[slot(c, me), :]

        @pl.when(t >= 2)
        def _():
            c = t - 2
            at = pl.ds(c * size, size)

            @pl.loop(1, frames)
            def _(i):
                source = lax.rem(me + i, frames)
                back_copy(c, source, source).wait_recv()

            stepped[at, :] += dot(obuf[at, :], w_tout[...])
            out_copy(c).start()

    @pl.loop(1, devices)
    def _(i):
        peer = lax.rem(mine + i, devices)
        stat_copy(peer, mine).wait_send()

    @pl.loop(0, chunks)
    def _(c):
        near_copy(c).wait_send()
        out_copy(c).wait()
        tok_copy(c).wait_send()

        @pl.when(relays)
        def _():
            far_copy(c).wait_send()

        @pl.loop(1, frames)
        def _(i):
            dest = lax.rem(me + i, frames)
            fwd_copy(c, dest, me).wait_send()
            back_copy(c, dest, me).wait_send()


def body(
    frames, rows,
    latent, norm_gain, time_kernel, space_norm, space_qkv, space_out, time_norm, time_qkv, time_out,
):
    held, row_count, col_count, channels = latent.shape
    pixels = held * row_count * col_count
    per_group = channels // GROUPS
    chunks = max(1, pixels // (16 * frames))
    size = pixels // chunks
    number = float(frames * rows * pixels * per_group)
    devices = frames * rows
    vmem = pl.BlockSpec(memory_space=pltpu.VMEM)
    hbm = pl.BlockSpec(memory_space=pl.ANY)

    def wide(n=pixels, kind=BF16, width=channels):
        return pltpu.VMEM((n, width), kind)

    dma = pltpu.SemaphoreType.DMA
    output = pl.pallas_call(
        functools.partial(kernel, frames, rows, chunks, number, per_group),
        out_shape=jax.ShapeDtypeStruct((pixels, channels), F32),
        in_specs=[hbm, vmem, hbm, vmem, hbm, hbm, vmem, hbm, hbm],
        out_specs=hbm,
        scratch_shapes=[
            wide(), wide(), wide(), wide(kind=F32), wide(), wide(), wide(), wide(2 * pixels), wide(2 * pixels),
            wide(), wide(), wide(), wide(),
            pltpu.VMEM((8, channels), F32),
            pltpu.VMEM((devices, 8, channels), F32),
            pltpu.VMEM((3, channels, channels), BF16),
            wide(channels, BF16, 3 * channels), wide(channels),
            wide(channels, BF16, 3 * channels), wide(channels),
            wide(size), wide(size), wide(size), wide(size),
            pltpu.VMEM((8, channels), F32),
            wide(channels),
            dma((8,)), dma((devices,)), dma((devices,)),
            dma((chunks,)), dma((chunks,)), dma((chunks,)), dma((chunks,)), dma((chunks,)), dma((chunks,)),
            dma((chunks, frames)), dma((chunks, frames)), dma((chunks, frames)), dma((chunks, frames)), dma((chunks,)),
        ],
        compiler_params=pltpu.CompilerParams(
            collective_id=0, has_side_effects=True, vmem_limit_bytes=60 * 1024 * 1024
        ),
    )(
        latent.reshape(pixels, channels), norm_gain, time_kernel, space_norm, space_qkv,
        space_out, time_norm, time_qkv, time_out,
    )
    return output.reshape(latent.shape)


def solution(mesh):
    frames, rows = mesh.shape["frame"], mesh.shape["row"]
    split = P(("groups", "frame"), "row", None, None)
    return jax.shard_map(
        functools.partial(body, frames, rows),
        mesh=mesh,
        in_specs=(split, P(), P(), P(), P(), P(), P(), P(), P()),
        out_specs=split,
        check_vma=False,
    )
```

```python
import functools

import jax
import jax.numpy as jnp
from jax import lax
from jax.experimental import pallas as pl
from jax.experimental.pallas import tpu as pltpu
from jax.sharding import PartitionSpec as P

HEADS = 10
GROUPS = 32
MESH = pl.DeviceIdType.MESH
F32 = jnp.float32
BF16 = jnp.bfloat16

epsilon = 1e-05


def layer_norm(inputs, gain):
    center = jnp.mean(inputs, axis=-1, keepdims=True)
    shifted = inputs - center
    spread = jnp.mean(shifted * shifted, axis=-1, keepdims=True)
    return (shifted * lax.rsqrt(spread + epsilon) * gain).astype(BF16)


def dot(a, b):
    return jnp.dot(a, b, preferred_element_type=F32)


def dot_nt(a, b):
    return lax.dot_general(a, b, (((1,), (1,)), ((), ())), preferred_element_type=F32)


def kernel(
    frames, rows, chunks, number, per_group,
    latent, norm_gain, time_kernel, space_norm, space_qkv, space_out, time_norm, time_qkv, time_out,
    out,
    own, near, far, stepped, tok_own, tok_other, q_all, k_all, v_all, nbuf, rbuf, abuf, obuf, part, stats,
    w_conv, w_sqkv, w_sout, w_tqkv, w_tout, att, q2, k2, v2, hid_scale, group_ones,
    w_sem, stat_send, stat_recv, near_send, near_recv, far_send, far_recv, tok_send, tok_recv,
    fwd_send, fwd_recv, back_send, back_recv, out_sem,
):
    me = lax.axis_index("frame")
    row = lax.axis_index("row")
    pixels, channels = own.shape
    size = pixels // chunks
    per = size // frames
    head = channels // HEADS
    pairs = HEADS // 2
    devices = frames * rows
    mine = me * rows + row
    odd = lax.rem(me, 2)
    partner = me + 1 - 2 * odd
    relay_to = me + 2 - 4 * odd
    far_from = me - 2 + 4 * odd
    relays = jnp.logical_and(relay_to >= 0, relay_to < frames)
    has_far = jnp.logical_and(far_from >= 0, far_from < frames)

    copies = [
        pltpu.make_async_copy(latent, own, w_sem.at[0]),
        pltpu.make_async_copy(time_kernel.at[1], w_conv.at[0], w_sem.at[1]),
        pltpu.make_async_copy(time_kernel.at[2 - 2 * odd], w_conv.at[1], w_sem.at[2]),
        pltpu.make_async_copy(time_kernel.at[2 * odd], w_conv.at[2], w_sem.at[3]),
        pltpu.make_async_copy(space_qkv, w_sqkv, w_sem.at[4]),
        pltpu.make_async_copy(space_out, w_sout, w_sem.at[5]),
        pltpu.make_async_copy(time_qkv, w_tqkv, w_sem.at[6]),
        pltpu.make_async_copy(time_out, w_tout, w_sem.at[7]),
    ]
    for copy in copies:
        copy.start()

    barrier = pltpu.get_barrier_semaphore()

    @pl.loop(1, devices)
    def _(i):
        peer = lax.rem(mine + i, devices)
        pl.semaphore_signal(
            barrier, inc=1, device_id={"frame": peer // rows, "row": lax.rem(peer, rows)}, device_id_type=MESH
        )

    copies[0].wait()
    first = jnp.zeros((1, channels), F32)
    second = jnp.zeros((1, channels), F32)
    for c in range(chunks):
        block = own[c * size : (c + 1) * size, :].astype(F32)
        first = first + jnp.sum(block, axis=0, keepdims=True)
        second = second + jnp.sum(block * block, axis=0, keepdims=True)
    part[...] = jnp.concatenate([first, second, jnp.zeros((6, channels), F32)], axis=0)
    down = lax.broadcasted_iota(jnp.int32, (channels, channels), 0)
    start = down - lax.rem(down, per_group)
    across = lax.broadcasted_iota(jnp.int32, (channels, channels), 1)
    inside = jnp.logical_and(across >= start, across < start + per_group)
    group_ones[...] = jnp.where(inside, 1.0, 0.0).astype(BF16)
    pl.semaphore_wait(barrier, devices - 1)

    def near_copy(j):
        at = pl.ds(j * size, size)
        return pltpu.make_async_remote_copy(
            latent.at[at], near.at[at], near_send.at[j], near_recv.at[j],
            device_id={"frame": partner}, device_id_type=MESH,
        )

    def far_copy(j):
        at = pl.ds(j * size, size)
        return pltpu.make_async_remote_copy(
            near.at[at], far.at[at], far_send.at[j], far_recv.at[j],
            device_id={"frame": lax.max(0, lax.min(relay_to, frames - 1))}, device_id_type=MESH,
        )

    def tok_copy(j):
        at = pl.ds(j * size, size)
        return pltpu.make_async_remote_copy(
            tok_own.at[at], tok_other.at[at], tok_send.at[j], tok_recv.at[j],
            device_id={"row": 1 - row}, device_id_type=MESH,
        )

    def stat_copy(peer, slot):
        return pltpu.make_async_remote_copy(
            part, stats.at[slot], stat_send.at[peer], stat_recv.at[slot],
            device_id={"frame": peer // rows, "row": lax.rem(peer, rows)}, device_id_type=MESH,
        )

    @pl.loop(1, devices)
    def _(i):
        peer = lax.rem(mine + i, devices)
        stat_copy(peer, mine).start()

    @pl.loop(0, chunks)
    def _(j):
        near_copy(j).start()

    stats[mine] = part[...]

    @pl.loop(1, devices)
    def _(i):
        source = lax.rem(mine + i, devices)
        stat_copy(source, source).wait_recv()

    total = jnp.sum(stats[...], axis=0)
    high = total.astype(BF16).astype(F32)
    middle = (total - high).astype(BF16).astype(F32)
    lowest = total - high - middle
    pieces = dot(jnp.concatenate([high, middle, lowest], axis=0).astype(BF16), group_ones[...])
    grouped = pieces[0:8] + pieces[8:16] + pieces[16:24]
    center = grouped[0:1] / number
    spread = grouped[1:2] / number - center * center
    hid_scale[0:1, :] = center
    hid_scale[1:2, :] = lax.rsqrt(spread + epsilon) * norm_gain[...].reshape(1, channels)

    def hidden(ref, c):
        block = ref[pl.ds(c * size, size), :].astype(F32)
        v = (block - hid_scale[0:1, :]) * hid_scale[1:2, :]
        return (v / (1.0 + jnp.exp(-v))).astype(BF16)

    copies[1].wait()

    @pl.loop(0, chunks)
    def _(c):
        at = pl.ds(c * size, size)
        stepped[at, :] = own[at, :].astype(F32) + dot(hidden(own, c), w_conv[0])

    for copy in copies[2:6]:
        copy.wait()

    scale = head ** (-0.5)

    @pl.loop(0, chunks + 2)
    def _(t):
        @pl.when(t < chunks)
        def _():
            near_copy(t).wait_recv()

            @pl.when(relays)
            def _():
                far_copy(t).start()

            at = pl.ds(t * size, size)
            stepped[at, :] += dot(hidden(near, t), w_conv[1])

        @pl.when(jnp.logical_and(t >= 1, t <= chunks))
        def _():
            c = t - 1
            at = pl.ds(c * size, size)

            @pl.when(has_far)
            def _():
                far_copy(c).wait_recv()
                stepped[at, :] += dot(hidden(far, c), w_conv[2])

            tok_own[at, :] = layer_norm(stepped[at, :], space_norm[...].reshape(1, channels))
            tok_copy(c).start()
            tokens = tok_own[at, :]
            q_all[at, :] = (dot(tokens, w_sqkv[:, :channels]) * scale).astype(BF16)
            k_all[at, :] = dot(tokens, w_sqkv[:, channels : 2 * channels]).astype(BF16)
            v_all[at, :] = dot(tokens, w_sqkv[:, 2 * channels :]).astype(BF16)

        @pl.when(t >= 2)
        def _():
            c = t - 2
            tok_copy(c).wait_recv()
            tokens = tok_other[pl.ds(c * size, size), :]
            to = pl.ds(pixels + c * size, size)
            k_all[to, :] = dot(tokens, w_sqkv[:, channels : 2 * channels]).astype(BF16)
            v_all[to, :] = dot(tokens, w_sqkv[:, 2 * channels :]).astype(BF16)

    for copy in copies[6:]:
        copy.wait()

    lane = lax.broadcasted_iota(jnp.int32, (1, 2 * head), 1)
    low = lane < head
    masks = (low.astype(F32).astype(BF16), (1.0 - low.astype(F32)).astype(BF16))

    def attend_pair(query, keys, values, same):
        both = jnp.concatenate([query * mask for mask in masks], axis=0)
        scores = dot_nt(both, keys)
        if same is not None:
            scores = jnp.where(same, scores, -jnp.inf)
        raised = jnp.exp(scores - jnp.max(scores, axis=-1, keepdims=True))
        weight_sum = jnp.sum(raised, axis=-1, keepdims=True)
        result = dot(raised.astype(BF16), values) / weight_sum
        return jnp.where(low, result[:size], result[size:]).astype(BF16)

    def slot(c, f):
        return pl.ds(pl.multiple_of(c * size + f * per, per), per)

    def fwd_copy(c, dest, source):
        return pltpu.make_async_remote_copy(
            nbuf.at[slot(c, dest)], rbuf.at[slot(c, source)],
            fwd_send.at[c, dest], fwd_recv.at[c, source],
            device_id={"frame": dest}, device_id_type=MESH,
        )

    def out_copy(c):
        at = pl.ds(c * size, size)
        return pltpu.make_async_copy(stepped.at[at], out.at[at], out_sem.at[c])

    def back_copy(c, dest, source):
        return pltpu.make_async_remote_copy(
            abuf.at[slot(c, dest)], obuf.at[slot(c, source)],
            back_send.at[c, dest], back_recv.at[c, source],
            device_id={"frame": dest}, device_id_type=MESH,
        )

    @pl.loop(0, chunks + 4)
    def _(t):
        @pl.when(t < chunks)
        def _():
            c = t
            at = pl.ds(c * size, size)
            for p in range(pairs):
                block = slice(p * 2 * head, (p + 1) * 2 * head)
                att[:, block] = attend_pair(q_all[at, block], k_all[:, block], v_all[:, block], None)
            spaced = stepped[at, :] + dot(att[...], w_sout[...])
            stepped[at, :] = spaced
            nbuf[at, :] = layer_norm(spaced, time_norm[...].reshape(1, channels))

            @pl.loop(1, frames)
            def _(i):
                fwd_copy(c, lax.rem(me + i, frames), me).start()

            rbuf[slot(c, me), :] = nbuf[slot(c, me), :]

        @pl.when(jnp.logical_and(t >= 2, t <= chunks + 1))
        def _():
            c = t - 2
            at = pl.ds(c * size, size)

            @pl.loop(1, frames)
            def _(i):
                source = lax.rem(me + i, frames)
                fwd_copy(c, source, source).wait_recv()

            tokens = rbuf[at, :]
            q2[...] = (dot(tokens, w_tqkv[:, :channels]) * scale).astype(BF16)
            k2[...] = dot(tokens, w_tqkv[:, channels : 2 * channels]).astype(BF16)
            v2[...] = dot(tokens, w_tqkv[:, 2 * channels :]).astype(BF16)
            across = lax.broadcasted_iota(jnp.int32, (2 * size, size), 1)
            down = lax.broadcasted_iota(jnp.int32, (2 * size, size), 0)
            same = lax.rem(across, per) == lax.rem(down, per)
            for p in range(pairs):
                block = slice(p * 2 * head, (p + 1) * 2 * head)
                abuf[at, block] = attend_pair(q2[:, block], k2[:, block], v2[:, block], same)

            @pl.loop(1, frames)
            def _(i):
                back_copy(c, lax.rem(me + i, frames), me).start()

            obuf[slot(c, me), :] = abuf[slot(c, me), :]

        @pl.when(t >= 4)
        def _():
            c = t - 4
            at = pl.ds(c * size, size)

            @pl.loop(1, frames)
            def _(i):
                source = lax.rem(me + i, frames)
                back_copy(c, source, source).wait_recv()

            stepped[at, :] += dot(obuf[at, :], w_tout[...])
            out_copy(c).start()

    @pl.loop(1, devices)
    def _(i):
        peer = lax.rem(mine + i, devices)
        stat_copy(peer, mine).wait_send()

    @pl.loop(0, chunks)
    def _(c):
        near_copy(c).wait_send()
        out_copy(c).wait()
        tok_copy(c).wait_send()

        @pl.when(relays)
        def _():
            far_copy(c).wait_send()

        @pl.loop(1, frames)
        def _(i):
            dest = lax.rem(me + i, frames)
            fwd_copy(c, dest, me).wait_send()
            back_copy(c, dest, me).wait_send()


def body(
    frames, rows,
    latent, norm_gain, time_kernel, space_norm, space_qkv, space_out, time_norm, time_qkv, time_out,
):
    held, row_count, col_count, channels = latent.shape
    pixels = held * row_count * col_count
    per_group = channels // GROUPS
    chunks = max(1, pixels // (16 * frames))
    size = pixels // chunks
    number = float(frames * rows * pixels * per_group)
    devices = frames * rows
    vmem = pl.BlockSpec(memory_space=pltpu.VMEM)
    hbm = pl.BlockSpec(memory_space=pl.ANY)

    def wide(n=pixels, kind=BF16, width=channels):
        return pltpu.VMEM((n, width), kind)

    dma = pltpu.SemaphoreType.DMA
    output = pl.pallas_call(
        functools.partial(kernel, frames, rows, chunks, number, per_group),
        out_shape=jax.ShapeDtypeStruct((pixels, channels), F32),
        in_specs=[hbm, vmem, hbm, vmem, hbm, hbm, vmem, hbm, hbm],
        out_specs=hbm,
        scratch_shapes=[
            wide(), wide(), wide(), wide(kind=F32), wide(), wide(), wide(), wide(2 * pixels), wide(2 * pixels),
            wide(), wide(), wide(), wide(),
            pltpu.VMEM((8, channels), F32),
            pltpu.VMEM((devices, 8, channels), F32),
            pltpu.VMEM((3, channels, channels), BF16),
            wide(channels, BF16, 3 * channels), wide(channels),
            wide(channels, BF16, 3 * channels), wide(channels),
            wide(size), wide(size), wide(size), wide(size),
            pltpu.VMEM((8, channels), F32),
            wide(channels),
            dma((8,)), dma((devices,)), dma((devices,)),
            dma((chunks,)), dma((chunks,)), dma((chunks,)), dma((chunks,)), dma((chunks,)), dma((chunks,)),
            dma((chunks, frames)), dma((chunks, frames)), dma((chunks, frames)), dma((chunks, frames)), dma((chunks,)),
        ],
        compiler_params=pltpu.CompilerParams(
            collective_id=0, has_side_effects=True, vmem_limit_bytes=60 * 1024 * 1024
        ),
    )(
        latent.reshape(pixels, channels), norm_gain, time_kernel, space_norm, space_qkv,
        space_out, time_norm, time_qkv, time_out,
    )
    return output.reshape(latent.shape)


def solution(mesh):
    frames, rows = mesh.shape["frame"], mesh.shape["row"]
    split = P(("groups", "frame"), "row", None, None)
    return jax.shard_map(
        functools.partial(body, frames, rows),
        mesh=mesh,
        in_specs=(split, P(), P(), P(), P(), P(), P(), P(), P()),
        out_specs=split,
        check_vma=False,
    )
```

```python
import functools

import jax
import jax.numpy as jnp
from jax import lax
from jax.experimental import pallas as pl
from jax.experimental.pallas import tpu as pltpu
from jax.sharding import PartitionSpec as P

HEADS = 10
GROUPS = 32
MESH = pl.DeviceIdType.MESH
F32 = jnp.float32
BF16 = jnp.bfloat16

epsilon = 1e-05


def layer_norm(inputs, gain):
    center = jnp.mean(inputs, axis=-1, keepdims=True)
    shifted = inputs - center
    spread = jnp.mean(shifted * shifted, axis=-1, keepdims=True)
    return (shifted * lax.rsqrt(spread + epsilon) * gain).astype(BF16)


def dot(a, b):
    return jnp.dot(a, b, preferred_element_type=F32)


def dot_nt(a, b):
    return lax.dot_general(a, b, (((1,), (1,)), ((), ())), preferred_element_type=F32)


def kernel(
    frames, rows, chunks, number, per_group,
    latent, norm_gain, time_kernel, space_norm, space_qkv, space_out, time_norm, time_qkv, time_out,
    out,
    own, near, far, stepped, tok_own, tok_other, q_all, k_all, v_all, nbuf, rbuf, abuf, obuf, part, stats,
    w_conv, w_sqkv, w_sout, w_tqkv, w_tout, att, q2, k2, v2, hid_scale, group_ones,
    w_sem, stat_send, stat_recv, near_send, near_recv, far_send, far_recv, tok_send, tok_recv,
    fwd_send, fwd_recv, back_send, back_recv, out_sem,
):
    me = lax.axis_index("frame")
    row = lax.axis_index("row")
    pixels, channels = own.shape
    size = pixels // chunks
    per = size // frames
    head = channels // HEADS
    pairs = HEADS // 2
    devices = frames * rows
    mine = me * rows + row
    odd = lax.rem(me, 2)
    partner = me + 1 - 2 * odd
    relay_to = me + 2 - 4 * odd
    far_from = me - 2 + 4 * odd
    relays = jnp.logical_and(relay_to >= 0, relay_to < frames)
    has_far = jnp.logical_and(far_from >= 0, far_from < frames)

    copies = [
        pltpu.make_async_copy(latent, own, w_sem.at[0]),
        pltpu.make_async_copy(time_kernel.at[1], w_conv.at[0], w_sem.at[1]),
        pltpu.make_async_copy(time_kernel.at[2 - 2 * odd], w_conv.at[1], w_sem.at[2]),
        pltpu.make_async_copy(time_kernel.at[2 * odd], w_conv.at[2], w_sem.at[3]),
        pltpu.make_async_copy(space_qkv, w_sqkv, w_sem.at[4]),
        pltpu.make_async_copy(space_out, w_sout, w_sem.at[5]),
        pltpu.make_async_copy(time_qkv, w_tqkv, w_sem.at[6]),
        pltpu.make_async_copy(time_out, w_tout, w_sem.at[7]),
    ]
    for copy in copies:
        copy.start()

    barrier = pltpu.get_barrier_semaphore()

    @pl.loop(1, devices)
    def _(i):
        peer = lax.rem(mine + i, devices)
        pl.semaphore_signal(
            barrier, inc=1, device_id={"frame": peer // rows, "row": lax.rem(peer, rows)}, device_id_type=MESH
        )

    copies[0].wait()
    first = jnp.zeros((1, channels), F32)
    second = jnp.zeros((1, channels), F32)
    for c in range(chunks):
        block = own[c * size : (c + 1) * size, :].astype(F32)
        first = first + jnp.sum(block, axis=0, keepdims=True)
        second = second + jnp.sum(block * block, axis=0, keepdims=True)
    part[...] = jnp.concatenate([first, second, jnp.zeros((6, channels), F32)], axis=0)
    down = lax.broadcasted_iota(jnp.int32, (channels, channels), 0)
    start = down - lax.rem(down, per_group)
    across = lax.broadcasted_iota(jnp.int32, (channels, channels), 1)
    inside = jnp.logical_and(across >= start, across < start + per_group)
    group_ones[...] = jnp.where(inside, 1.0, 0.0).astype(BF16)
    pl.semaphore_wait(barrier, devices - 1)

    def near_copy(j):
        at = pl.ds(j * size, size)
        return pltpu.make_async_remote_copy(
            latent.at[at], near.at[at], near_send.at[j], near_recv.at[j],
            device_id={"frame": partner}, device_id_type=MESH,
        )

    def far_copy(j):
        at = pl.ds(j * size, size)
        return pltpu.make_async_remote_copy(
            near.at[at], far.at[at], far_send.at[j], far_recv.at[j],
            device_id={"frame": lax.max(0, lax.min(relay_to, frames - 1))}, device_id_type=MESH,
        )

    def tok_copy(j):
        at = pl.ds(j * size, size)
        return pltpu.make_async_remote_copy(
            tok_own.at[at], tok_other.at[at], tok_send.at[j], tok_recv.at[j],
            device_id={"row": 1 - row}, device_id_type=MESH,
        )

    def stat_copy(peer, slot):
        return pltpu.make_async_remote_copy(
            part, stats.at[slot], stat_send.at[peer], stat_recv.at[slot],
            device_id={"frame": peer // rows, "row": lax.rem(peer, rows)}, device_id_type=MESH,
        )

    @pl.loop(1, devices)
    def _(i):
        peer = lax.rem(mine + i, devices)
        stat_copy(peer, mine).start()

    @pl.loop(0, chunks)
    def _(j):
        near_copy(j).start()

    stats[mine] = part[...]

    @pl.loop(1, devices)
    def _(i):
        source = lax.rem(mine + i, devices)
        stat_copy(source, source).wait_recv()

    total = jnp.sum(stats[...], axis=0)
    high = total.astype(BF16).astype(F32)
    middle = (total - high).astype(BF16).astype(F32)
    lowest = total - high - middle
    pieces = dot(jnp.concatenate([high, middle, lowest], axis=0).astype(BF16), group_ones[...])
    grouped = pieces[0:8] + pieces[8:16] + pieces[16:24]
    center = grouped[0:1] / number
    spread = grouped[1:2] / number - center * center
    hid_scale[0:1, :] = center
    hid_scale[1:2, :] = lax.rsqrt(spread + epsilon) * norm_gain[...].reshape(1, channels)

    def hidden(ref, c, size=size):
        block = ref[pl.ds(c * size, size), :].astype(F32)
        v = (block - hid_scale[0:1, :]) * hid_scale[1:2, :]
        return (v / (1.0 + jnp.exp(-v))).astype(BF16)

    copies[1].wait()

    half = pixels // 2

    @pl.loop(0, 2)
    def _(c):
        at = pl.ds(c * half, half)
        stepped[at, :] = own[at, :].astype(F32) + dot(hidden(own, c, half), w_conv[0])

    for copy in copies[2:6]:
        copy.wait()

    scale = head ** (-0.5)

    @pl.loop(0, chunks + 2)
    def _(t):
        @pl.when(t < chunks)
        def _():
            near_copy(t).wait_recv()

            @pl.when(relays)
            def _():
                far_copy(t).start()

            at = pl.ds(t * size, size)
            stepped[at, :] += dot(hidden(near, t), w_conv[1])

        @pl.when(t >= 2)
        def _():
            c = t - 2
            tok_copy(c).wait_recv()
            tokens = tok_other[pl.ds(c * size, size), :]
            to = pl.ds(pixels + c * size, size)
            k_all[to, :] = dot(tokens, w_sqkv[:, channels : 2 * channels]).astype(BF16)
            v_all[to, :] = dot(tokens, w_sqkv[:, 2 * channels :]).astype(BF16)

        @pl.when(jnp.logical_and(t >= 1, t <= chunks))
        def _():
            c = t - 1
            at = pl.ds(c * size, size)

            @pl.when(has_far)
            def _():
                far_copy(c).wait_recv()
                stepped[at, :] += dot(hidden(far, c), w_conv[2])

            tok_own[at, :] = layer_norm(stepped[at, :], space_norm[...].reshape(1, channels))
            tok_copy(c).start()
            tokens = tok_own[at, :]
            q_all[at, :] = (dot(tokens, w_sqkv[:, :channels]) * scale).astype(BF16)
            k_all[at, :] = dot(tokens, w_sqkv[:, channels : 2 * channels]).astype(BF16)
            v_all[at, :] = dot(tokens, w_sqkv[:, 2 * channels :]).astype(BF16)

    for copy in copies[6:]:
        copy.wait()

    lane = lax.broadcasted_iota(jnp.int32, (1, 2 * head), 1)
    low = lane < head
    masks = (low.astype(F32).astype(BF16), (1.0 - low.astype(F32)).astype(BF16))

    def attend_pair(query, keys, values, same):
        both = jnp.concatenate([query * mask for mask in masks], axis=0)
        scores = dot_nt(both, keys)
        if same is not None:
            scores = jnp.where(same, scores, -jnp.inf)
        raised = jnp.exp(scores - jnp.max(scores, axis=-1, keepdims=True))
        weight_sum = jnp.sum(raised, axis=-1, keepdims=True)
        result = dot(raised.astype(BF16), values) / weight_sum
        return jnp.where(low, result[:size], result[size:]).astype(BF16)

    def slot(c, f):
        return pl.ds(pl.multiple_of(c * size + f * per, per), per)

    def fwd_copy(c, dest, source):
        return pltpu.make_async_remote_copy(
            nbuf.at[slot(c, dest)], rbuf.at[slot(c, source)],
            fwd_send.at[c, dest], fwd_recv.at[c, source],
            device_id={"frame": dest}, device_id_type=MESH,
        )

    def out_copy(c):
        at = pl.ds(c * size, size)
        return pltpu.make_async_copy(stepped.at[at], out.at[at], out_sem.at[c])

    def back_copy(c, dest, source):
        return pltpu.make_async_remote_copy(
            abuf.at[slot(c, dest)], obuf.at[slot(c, source)],
            back_send.at[c, dest], back_recv.at[c, source],
            device_id={"frame": dest}, device_id_type=MESH,
        )

    @pl.loop(0, chunks + 4)
    def _(t):
        @pl.when(t < chunks)
        def _():
            c = t
            at = pl.ds(c * size, size)
            for p in range(pairs):
                block = slice(p * 2 * head, (p + 1) * 2 * head)
                att[:, block] = attend_pair(q_all[at, block], k_all[:, block], v_all[:, block], None)
            spaced = stepped[at, :] + dot(att[...], w_sout[...])
            stepped[at, :] = spaced
            nbuf[at, :] = layer_norm(spaced, time_norm[...].reshape(1, channels))

            @pl.loop(1, frames)
            def _(i):
                fwd_copy(c, lax.rem(me + i, frames), me).start()

            rbuf[slot(c, me), :] = nbuf[slot(c, me), :]

        @pl.when(jnp.logical_and(t >= 2, t <= chunks + 1))
        def _():
            c = t - 2
            at = pl.ds(c * size, size)

            @pl.loop(1, frames)
            def _(i):
                source = lax.rem(me + i, frames)
                fwd_copy(c, source, source).wait_recv()

            tokens = rbuf[at, :]
            q2[...] = (dot(tokens, w_tqkv[:, :channels]) * scale).astype(BF16)
            k2[...] = dot(tokens, w_tqkv[:, channels : 2 * channels]).astype(BF16)
            v2[...] = dot(tokens, w_tqkv[:, 2 * channels :]).astype(BF16)
            across = lax.broadcasted_iota(jnp.int32, (2 * size, size), 1)
            down = lax.broadcasted_iota(jnp.int32, (2 * size, size), 0)
            same = lax.rem(across, per) == lax.rem(down, per)
            for p in range(pairs):
                block = slice(p * 2 * head, (p + 1) * 2 * head)
                abuf[at, block] = attend_pair(q2[:, block], k2[:, block], v2[:, block], same)

            @pl.loop(1, frames)
            def _(i):
                back_copy(c, lax.rem(me + i, frames), me).start()

            obuf[slot(c, me), :] = abuf[slot(c, me), :]

        @pl.when(t >= 4)
        def _():
            c = t - 4
            at = pl.ds(c * size, size)

            @pl.loop(1, frames)
            def _(i):
                source = lax.rem(me + i, frames)
                back_copy(c, source, source).wait_recv()

            stepped[at, :] += dot(obuf[at, :], w_tout[...])
            out_copy(c).start()

    @pl.loop(1, devices)
    def _(i):
        peer = lax.rem(mine + i, devices)
        stat_copy(peer, mine).wait_send()

    @pl.loop(0, chunks)
    def _(c):
        near_copy(c).wait_send()
        out_copy(c).wait()
        tok_copy(c).wait_send()

        @pl.when(relays)
        def _():
            far_copy(c).wait_send()

        @pl.loop(1, frames)
        def _(i):
            dest = lax.rem(me + i, frames)
            fwd_copy(c, dest, me).wait_send()
            back_copy(c, dest, me).wait_send()


def body(
    frames, rows,
    latent, norm_gain, time_kernel, space_norm, space_qkv, space_out, time_norm, time_qkv, time_out,
):
    held, row_count, col_count, channels = latent.shape
    pixels = held * row_count * col_count
    per_group = channels // GROUPS
    chunks = max(1, pixels // (16 * frames))
    size = pixels // chunks
    number = float(frames * rows * pixels * per_group)
    devices = frames * rows
    vmem = pl.BlockSpec(memory_space=pltpu.VMEM)
    hbm = pl.BlockSpec(memory_space=pl.ANY)

    def wide(n=pixels, kind=BF16, width=channels):
        return pltpu.VMEM((n, width), kind)

    dma = pltpu.SemaphoreType.DMA
    output = pl.pallas_call(
        functools.partial(kernel, frames, rows, chunks, number, per_group),
        out_shape=jax.ShapeDtypeStruct((pixels, channels), F32),
        in_specs=[hbm, vmem, hbm, vmem, hbm, hbm, vmem, hbm, hbm],
        out_specs=hbm,
        scratch_shapes=[
            wide(), wide(), wide(), wide(kind=F32), wide(), wide(), wide(), wide(2 * pixels), wide(2 * pixels),
            wide(), wide(), wide(), wide(),
            pltpu.VMEM((8, channels), F32),
            pltpu.VMEM((devices, 8, channels), F32),
            pltpu.VMEM((3, channels, channels), BF16),
            wide(channels, BF16, 3 * channels), wide(channels),
            wide(channels, BF16, 3 * channels), wide(channels),
            wide(size), wide(size), wide(size), wide(size),
            pltpu.VMEM((8, channels), F32),
            wide(channels),
            dma((8,)), dma((devices,)), dma((devices,)),
            dma((chunks,)), dma((chunks,)), dma((chunks,)), dma((chunks,)), dma((chunks,)), dma((chunks,)),
            dma((chunks, frames)), dma((chunks, frames)), dma((chunks, frames)), dma((chunks, frames)), dma((chunks,)),
        ],
        compiler_params=pltpu.CompilerParams(
            collective_id=0, has_side_effects=True, vmem_limit_bytes=60 * 1024 * 1024
        ),
    )(
        latent.reshape(pixels, channels), norm_gain, time_kernel, space_norm, space_qkv,
        space_out, time_norm, time_qkv, time_out,
    )
    return output.reshape(latent.shape)


def solution(mesh):
    frames, rows = mesh.shape["frame"], mesh.shape["row"]
    split = P(("groups", "frame"), "row", None, None)
    return jax.shard_map(
        functools.partial(body, frames, rows),
        mesh=mesh,
        in_specs=(split, P(), P(), P(), P(), P(), P(), P(), P()),
        out_specs=split,
        check_vma=False,
    )
```
